32 devices in a mesh: dp: 16 (over z, x, core), rep: 2 (over y).
Axes of the slice: x: 2, y: 2, z: 4, core: 2. Of those that a mesh axis runs over, the one named last changes fastest.
Arguments:
- learn_residual: bfloat16 [20480, 1024], P(('dp', 'rep')), may hold values from -6 to 6
- learn_hidden: bfloat16 [20480, 4096], P(('dp', 'rep')), may hold values from -6 to 6
- fresh_residual: bfloat16 [20480, 1024], P(('dp', 'rep')), may hold values from -6 to 6
- fresh_hidden: bfloat16 [20480, 4096], P(('dp', 'rep')), may hold values from -6 to 6
- down_weight: bfloat16 [4096, 1024], P('dp'), may hold values from -0.09375 to 0.09375
- head_weight: bfloat16 [1024, 19], replicated, may hold values from -0.1875 to 0.1875
- norm_gain: bfloat16 [1024], replicated, may hold values from 0.099609375 to 1.8984375
- actions: int32 [256, 80], P(('dp', 'rep')), may hold values from 0 to 17
- behaviour_logits: float32 [20480, 18], P(('dp', 'rep')), may hold values from -6 to 6
- rewards: float32 [256, 80], P(('dp', 'rep')), may hold values from -6 to 6
- episode_done: int32 [256, 80], P(('dp', 'rep')), may hold values 0 or 1
- lengths: int32 [256], P(('dp', 'rep')), may hold values from 40 to 80, as said below
- bootstrap: float32 [256], P(('dp', 'rep')), may hold values from -6 to 6
Outputs:
- fresh_policy: float32 [20480, 19], P(('dp', 'rep'))
- learn_targets: float32 [256, 80], P(('dp', 'rep'))
- hidden_grad: bfloat16 [20480, 4096], P(('dp', 'rep'))
- down_grad: float32 [4096, 1024], P('dp')
- head_grad: float32 [1024, 19], replicated
- gain_grad: float32 [1024], replicated
The draws below stay inside these ranges and needn't reach their ends.
Inputs may be any that keep to these rules, and one draw needn't show every extreme that they name: `lengths`: on at least one device all 8 trajectories of that device have the full 80 steps.
All inputs are finite; a program needn't handle non-finite values. No bound on the sum of `episode_done` on one device may be relied on, other than what follows from the above.
Results may differ from the reference program's by a relative error of at most 0.0049.
Values may be sent and summed in bfloat16 or wider, within the bound.
A program may use at most 128 MiB of HBM per device.

```python
import jax
import jax.numpy as jnp
from jax import lax

D = 1024
FF = 4096
ACTIONS = 18
STEPS = 80
TRAJ_DEV = 8
OUTS = 19
TRAJ = 256
ROWS = 20480


def draw_lengths(key, part):
    base_key, pick_key = jax.random.split(jax.random.fold_in(key, 7))
    drawn = jax.random.randint(base_key, (TRAJ,), STEPS // 2, STEPS + 1)
    chosen_block = jax.random.randint(pick_key, (), 0, TRAJ // TRAJ_DEV)
    blocks = jnp.arange(TRAJ, dtype=jnp.int32) // TRAJ_DEV
    return jnp.where(blocks == chosen_block, STEPS, drawn).astype(jnp.int32)


def place_ends(array, own_key, smallest, high):
    longest = array.shape.index(max(array.shape))
    spots = []
    for shift in (0, 1):
        where = [jax.random.randint(jax.random.fold_in(own_key, axis), (), 0, length) for axis, length in enumerate(array.shape)]
        where[longest] = (where[longest] + shift) % array.shape[longest]
        spots.append(tuple(where))
    return array.at[spots[0]].set(smallest).at[spots[1]].set(high)


def with_spikes(result, stream_key, source, target, parts, factor):
    def block_of(axis_at):
        return (jnp.arange(result.shape[axis_at]) // (result.shape[axis_at] // parts)).reshape((-1,) + (1,) * (result.ndim - 1 - axis_at))

    one_side = jax.random.permutation(stream_key, parts)[block_of(target)]
    second = (block_of(target) + parts // 2) % parts
    return jnp.where((block_of(source) == one_side) | (block_of(source) == second), factor * result, result)


def block_scale(rng, dims, cuts, least, top_value):
    factor_of = 1.0
    for axis_at, blocks in cuts:
        heights = jax.random.uniform(jax.random.fold_in(jax.random.fold_in(rng, 6), axis_at), (blocks,), jnp.float32, least / len(cuts), top_value / len(cuts))
        factor_of = factor_of * jnp.repeat(jnp.exp(heights), dims[axis_at] // blocks).reshape((-1,) + (1,) * (len(dims) - 1 - axis_at))
    return factor_of


def bell_draw(own_key, shape, width, limit, cuts=(), held_as=jnp.bfloat16):
    array = width * jax.random.normal(own_key, shape, jnp.float32)
    if cuts:
        array = array * block_scale(own_key, shape, cuts, -0.22, 0.18)
    return jnp.clip(array, -limit, limit).astype(held_as)


def gaussian_with(rng, dims, deviation, bound, cuts, heavy, kind=jnp.bfloat16):
    result = deviation * jax.random.normal(rng, dims, jnp.float32)
    if cuts:
        result = result * block_scale(rng, dims, cuts, -0.22, 0.18)
    return jnp.clip(with_spikes(result, jax.random.fold_in(rng, 3), *heavy), -bound, bound).astype(kind)


def setup_inputs(seed: int = 0) -> dict:
    seeds = jax.random.split(jax.random.key(seed), 14)
    return {
        "learn_residual": bell_draw(seeds[0], (ROWS, D), 1.0, 6.0, ((0, 32),)),
        "learn_hidden": gaussian_with(seeds[1], (ROWS, FF), 1.0, 6.0, ((0, 32),), (0, 1, 32, 2.75)),
        "fresh_residual": bell_draw(seeds[2], (ROWS, D), 1.0, 6.0, ((0, 32),)),
        "fresh_hidden": bell_draw(seeds[3], (ROWS, FF), 1.0, 6.0, ((0, 32),)),
        "down_weight": bell_draw(seeds[4], (FF, D), FF ** -0.5, 0.09375, ((0, 16),)),
        "head_weight": bell_draw(seeds[5], (D, OUTS), D ** -0.5, 0.1875),
        "norm_gain": jnp.clip(1.0 + 0.18 * jax.random.normal(seeds[6], (D,), jnp.float32), 0.099609375, 1.8984375).astype(jnp.bfloat16),
        "actions": place_ends(jax.random.randint(seeds[7], (TRAJ, STEPS), 0, ACTIONS), jax.random.fold_in(seeds[7], 1), 0, ACTIONS - 1).astype(jnp.int32),
        "behaviour_logits": bell_draw(seeds[8], (ROWS, ACTIONS), 1.0, 6.0, ((0, 32),), jnp.float32),
        "rewards": bell_draw(seeds[9], (TRAJ, STEPS), 1.0, 6.0, ((0, 32),), jnp.float32),
        "episode_done": place_ends((jax.random.randint(seeds[10], (TRAJ, STEPS), 0, 20) < 1).astype(jnp.int32), jax.random.fold_in(seeds[10], 1), 0, 1),
        "lengths": draw_lengths(jax.random.fold_in(seeds[13], 71), 0),
        "bootstrap": bell_draw(seeds[12], (TRAJ,), 1.0, 6.0, ((0, 32),), jnp.float32),
    }


DISCOUNT = 0.99
BASELINE_COST = 0.5
ENTROPY_COST = 0.05
EPSILON = 1e-05

def normalize(features, gain_vector):
    inverse_rms = lax.rsqrt(lax.optimization_barrier(jnp.mean(features * features, axis=1, keepdims=True)) + EPSILON)
    return features * inverse_rms * gain_vector[None, :]

def head_outputs(features, head_matrix, gain_vector):
    return jnp.dot(normalize(features, gain_vector), head_matrix, precision=lax.Precision.HIGHEST)

def log_policy(logits):
    return logits - jnp.log(lax.optimization_barrier(jnp.sum(jnp.exp(logits), axis=-1, keepdims=True)))

def trace_returns(errors, traces):

    def step_back(running, step_inputs):
        error_now, trace_now = step_inputs
        running = error_now + trace_now * running
        return (running, running)
    start = jnp.zeros((errors.shape[0],), jnp.float32)
    _, corrections = lax.scan(step_back, start, (errors.T, traces.T), reverse=True)
    return corrections.T

def learner_loss(features, head_matrix, gain_vector, actions, behaviour_logits, rewards, episode_done, lengths, bootstrap):
    trajectories = actions.shape[0]
    outputs = head_outputs(features, head_matrix, gain_vector)
    logprob = log_policy(outputs[:, :ACTIONS])
    values = outputs[:, ACTIONS].reshape(trajectories, STEPS)
    one_hot = (actions.reshape(-1)[:, None] == jnp.arange(ACTIONS, dtype=jnp.int32)[None, :]).astype(jnp.float32)
    taken = lax.optimization_barrier(jnp.sum(logprob * one_hot, axis=1)).reshape(trajectories, STEPS)
    behaved = lax.optimization_barrier(jnp.sum(log_policy(behaviour_logits) * one_hot, axis=1)).reshape(trajectories, STEPS)
    entropy = -lax.optimization_barrier(jnp.sum(jnp.exp(logprob) * logprob, axis=1)).reshape(trajectories, STEPS)
    clipped_ratio = jnp.minimum(1.0, jnp.exp(lax.stop_gradient(taken) - behaved))
    positions = jnp.arange(STEPS, dtype=jnp.int32)[None, :]
    inside = positions < lengths[:, None]
    final_step = positions == lengths[:, None] - 1
    discounts = DISCOUNT * (1.0 - episode_done.astype(jnp.float32))
    baseline = lax.stop_gradient(values)
    empty_column = jnp.zeros((trajectories, 1), jnp.float32)
    next_value = jnp.concatenate([baseline[:, 1:], empty_column], axis=1)
    next_value = jnp.where(final_step, bootstrap[:, None], next_value)
    errors = jnp.where(inside, clipped_ratio * (rewards + discounts * next_value - baseline), 0.0)
    traces = jnp.where(inside, discounts * clipped_ratio, 0.0)
    targets = baseline + trace_returns(errors, traces)
    next_target = jnp.concatenate([targets[:, 1:], empty_column], axis=1)
    next_target = jnp.where(final_step, bootstrap[:, None], next_target)
    advantage = clipped_ratio * (rewards + discounts * next_target - baseline)
    per_step = -advantage * taken + 0.5 * BASELINE_COST * (targets - values) ** 2 - ENTROPY_COST * entropy
    total_loss = jnp.sum(jnp.where(inside, per_step, 0.0)) / (TRAJ_DEV * STEPS)
    return (total_loss, targets)

def reference(learn_residual, learn_hidden, fresh_residual, fresh_hidden, down_weight, head_weight, norm_gain, actions, behaviour_logits, rewards, episode_done, lengths, bootstrap):
    learn_stream = learn_residual.astype(jnp.float32) + jnp.dot(learn_hidden, down_weight, preferred_element_type=jnp.float32)
    fresh_stream = fresh_residual.astype(jnp.float32) + jnp.dot(fresh_hidden, down_weight, preferred_element_type=jnp.float32)
    head_matrix = head_weight.astype(jnp.float32)
    gain_vector = norm_gain.astype(jnp.float32)
    fresh_policy = head_outputs(fresh_stream, head_matrix, gain_vector)

    def loss_of(features, head_values, gain_values):
        return learner_loss(features, head_values, gain_values, actions, behaviour_logits, rewards, episode_done, lengths, bootstrap)
    total_loss, pullback, targets = jax.vjp(loss_of, learn_stream, head_matrix, gain_vector, has_aux=True)
    stream_grad, head_grad, gain_grad = pullback(jnp.ones_like(total_loss))
    rounded = stream_grad.astype(jnp.bfloat16)
    down_grad = lax.dot_general(learn_hidden, rounded, (((0,), (0,)), ((), ())), preferred_element_type=jnp.float32)
    hidden_grad = lax.dot_general(rounded, down_weight, (((1,), (1,)), ((), ())), preferred_element_type=jnp.float32).astype(jnp.bfloat16)
    return (fresh_policy, targets, hidden_grad, down_grad, head_grad, gain_grad)
```

```python
import functools

import jax
import jax.numpy as jnp
from jax import lax
from jax.experimental import pallas as pl
from jax.experimental.pallas import tpu as pltpu
from jax.sharding import PartitionSpec as P

ACTIONS = 18
STEPS = 80
TRAJ_DEV = 8


DISCOUNT = 0.99
BASELINE_COST = 0.5
ENTROPY_COST = 0.05
EPSILON = 1e-05


def normalize(features, gain_vector):
    inverse_rms = lax.rsqrt(jnp.mean(features * features, axis=1, keepdims=True) + EPSILON)
    return features * inverse_rms * gain_vector[None, :]


def head_outputs(features, head_matrix, gain_vector):
    return jnp.dot(normalize(features, gain_vector), head_matrix, precision=lax.Precision.HIGHEST)


def log_policy(logits):
    return logits - jnp.log(jnp.sum(jnp.exp(logits), axis=-1, keepdims=True))


def compose_steps(earlier, later):
    return (earlier[0] * later[0], later[1] + later[0] * earlier[1])


def trace_returns(errors, traces):
    _, corrections = lax.associative_scan(compose_steps, (traces, errors), reverse=True, axis=1)
    return corrections


def learner_loss(
    features,
    head_matrix,
    gain_vector,
    actions,
    behaviour_logits,
    rewards,
    episode_done,
    lengths,
    bootstrap,
):
    trajectories = actions.shape[0]
    outputs = head_outputs(features, head_matrix, gain_vector)
    logprob = log_policy(outputs[:, :ACTIONS])
    values = outputs[:, ACTIONS].reshape(trajectories, STEPS)
    one_hot = (
        actions.reshape(-1)[:, None] == jnp.arange(ACTIONS, dtype=jnp.int32)[None, :]
    ).astype(jnp.float32)
    taken = jnp.sum(logprob * one_hot, axis=1).reshape(trajectories, STEPS)
    behaved = jnp.sum(log_policy(behaviour_logits) * one_hot, axis=1).reshape(trajectories, STEPS)
    entropy = -jnp.sum(jnp.exp(logprob) * logprob, axis=1).reshape(trajectories, STEPS)
    clipped_ratio = jnp.minimum(1.0, jnp.exp(lax.stop_gradient(taken) - behaved))
    positions = jnp.arange(STEPS, dtype=jnp.int32)[None, :]
    inside = positions < lengths[:, None]
    final_step = positions == lengths[:, None] - 1
    discounts = DISCOUNT * (1.0 - episode_done.astype(jnp.float32))
    baseline = lax.stop_gradient(values)
    empty_column = jnp.zeros((trajectories, 1), jnp.float32)
    next_value = jnp.concatenate([baseline[:, 1:], empty_column], axis=1)
    next_value = jnp.where(final_step, bootstrap[:, None], next_value)
    errors = jnp.where(inside, clipped_ratio * (rewards + discounts * next_value - baseline), 0.0)
    traces = jnp.where(inside, discounts * clipped_ratio, 0.0)
    targets = baseline + trace_returns(errors, traces)
    next_target = jnp.concatenate([targets[:, 1:], empty_column], axis=1)
    next_target = jnp.where(final_step, bootstrap[:, None], next_target)
    advantage = clipped_ratio * (rewards + discounts * next_target - baseline)
    per_step = (
        -advantage * taken + 0.5 * BASELINE_COST * (targets - values) ** 2 - ENTROPY_COST * entropy
    )
    total_loss = jnp.sum(jnp.where(inside, per_step, 0.0)) / (TRAJ_DEV * STEPS)
    return (total_loss, targets)


def copy_block(index_ref, in_ref, out_ref):
    out_ref[...] = in_ref[...]


def pick_columns(array, order, width):
    rows, total = array.shape
    count = total // width
    if width % 128:
        picked = jnp.take(array.reshape(rows, count, width), order, axis=1)
        return picked.reshape(rows, total)
    return pl.pallas_call(
        copy_block,
        out_shape=jax.ShapeDtypeStruct(array.shape, array.dtype),
        grid_spec=pltpu.PrefetchScalarGridSpec(
            num_scalar_prefetch=1,
            grid=(count,),
            in_specs=[pl.BlockSpec((rows, width), lambda j, index: (0, index[j]))],
            out_specs=pl.BlockSpec((rows, width), lambda j, index: (0, j)),
        ),
        cost_estimate=pl.CostEstimate(
            flops=0, bytes_accessed=2 * array.size * array.dtype.itemsize, transcendentals=0
        ),
    )(order, array)


def copy_either(half, index_ref, first_ref, second_ref, out_ref):
    j = pl.program_id(0)

    @pl.when(j < half)
    def _():
        out_ref[...] = first_ref[...]

    @pl.when(j >= half)
    def _():
        out_ref[...] = second_ref[...]


def place_rows(first, second, order, height):
    half = first.shape[0] // height
    width = first.shape[1]
    return pl.pallas_call(
        lambda *refs: copy_either(half, *refs),
        out_shape=jax.ShapeDtypeStruct((2 * first.shape[0], width), first.dtype),
        grid_spec=pltpu.PrefetchScalarGridSpec(
            num_scalar_prefetch=1,
            grid=(2 * half,),
            in_specs=[
                pl.BlockSpec((height, width), lambda j, index: (jnp.minimum(j, half - 1), 0)),
                pl.BlockSpec((height, width), lambda j, index: (jnp.maximum(j - half, 0), 0)),
            ],
            out_specs=pl.BlockSpec((height, width), lambda j, index: (index[j], 0)),
        ),
        cost_estimate=pl.CostEstimate(
            flops=0, bytes_accessed=4 * first.size * first.dtype.itemsize, transcendentals=0
        ),
    )(order, first, second)


def local(count, learn_residual,
    learn_hidden,
    fresh_residual,
    fresh_hidden,
    down_weight,
    head_weight,
    norm_gain,
    actions,
    behaviour_logits,
    rewards,
    episode_done,
    lengths,
    bootstrap):
    slow = count // 4
    half_rows = down_weight.shape[0] // 2
    width = down_weight.shape[1]
    cols = width // 2
    bf16, f32 = jnp.bfloat16, jnp.float32

    def flip(array, bit):
        return lax.ppermute(array, "dp", [(i, i ^ bit) for i in range(count)])

    def turn(array, steps):
        return lax.ppermute(array, "dp", [(i, (i + 4 * steps) % count) for i in range(count)])

    def other(array):
        return lax.ppermute(array, "rep", [(0, 1), (1, 0)])

    me = lax.axis_index("dp")
    my_rep = lax.axis_index("rep")
    my_slow, my_mid, my_core = me // 4, (me // 2) % 2, me % 2
    place = jnp.arange(count * 2, dtype=jnp.int32)
    s_slow = place % slow
    s_rep = (place // slow) % 2
    s_mid = (place // (slow * 2)) % 2
    s_core = place // (slow * 4)
    block = ((my_slow + s_slow) % slow) * 4 + ((my_mid + s_mid) % 2) * 2 + (my_core + s_core) % 2
    order = (block * 2 + (my_rep + s_rep) % 2).astype(jnp.int32)

    head_matrix = head_weight.astype(f32)
    gain_vector = norm_gain.astype(f32)
    ordered = pick_columns(learn_hidden, order, half_rows)

    piece = lax.dynamic_slice_in_dim(down_weight, my_rep * half_rows, half_rows, 0)
    ring = [piece]
    for _ in range(slow - 1):
        ring.append(turn(ring[-1], -1))
    line = jnp.concatenate(ring, axis=0)
    first, second = line[:, :cols], line[:, cols:]
    first_rep = other(first)
    second_mid = flip(second, 2)
    first = jnp.concatenate([first, first_rep], axis=0)
    second = jnp.concatenate([second, second_mid], axis=0)
    first_mid = flip(first, 2)
    second_rep = other(second)
    first = jnp.concatenate([first, first_mid], axis=0)
    step = slow * half_rows
    second = jnp.concatenate(
        [second[:step], second_rep[:step], second[step:], second_rep[step:]], axis=0
    )
    own_weight = jnp.concatenate([first, second], axis=1)
    far_weight = flip(own_weight, 1)
    depth = own_weight.shape[0]

    learn_stream = learn_residual.astype(f32) + (
        jnp.dot(ordered[:, :depth], own_weight, preferred_element_type=f32)
        + jnp.dot(ordered[:, depth:], far_weight, preferred_element_type=f32)
    )

    def loss_of(features, head_values, gain_values):
        return learner_loss(
            features,
            head_values,
            gain_values,
            actions,
            behaviour_logits,
            rewards,
            episode_done,
            lengths,
            bootstrap,
        )

    total_loss, pullback, targets = jax.vjp(
        loss_of, learn_stream, head_matrix, gain_vector, has_aux=True
    )
    stream_grad, head_local, gain_local = pullback(jnp.ones_like(total_loss))
    rounded = stream_grad.astype(bf16)

    def grad_of(hidden_part, columns):
        return lax.dot_general(
            hidden_part, columns, (((0,), (0,)), ((), ())), preferred_element_type=f32
        )

    sides = (rounded[:, :cols], rounded[:, cols:])
    sent = [flip(grad_of(ordered[:, depth:], side).astype(bf16), 1) for side in sides]
    part = [
        grad_of(ordered[:, :depth], side) + got.astype(f32) for side, got in zip(sides, sent)
    ]
    a, b = part
    a = a.reshape(2, 2, step, cols)
    b = b.reshape(2, 2, step, cols)
    a_got = flip(a[1].astype(bf16), 2)
    b_got = other(b[:, 1].astype(bf16))
    a = a[0] + a_got.astype(f32)
    b = b[:, 0] + b_got.astype(f32)
    a_got = other(a[1].astype(bf16))
    b_got = flip(b[1].astype(bf16), 2)
    a = a[0] + a_got.astype(f32)
    b = b[0] + b_got.astype(f32)
    done = []
    for whole in (a, b):
        whole = whole.reshape(slow, half_rows, cols)
        narrow = whole.astype(bf16)
        arrived = [turn(narrow[s], s) for s in range(1, slow)]
        total = whole[0]
        for got in arrived:
            total = total + got.astype(f32)
        done.append(lax.reduce_precision(total, 8, 7))
    mine = jnp.concatenate(done, axis=1)
    theirs = other(mine.astype(bf16)).astype(f32)
    low = jnp.where(my_rep == 0, mine, theirs)
    high = jnp.where(my_rep == 0, theirs, mine)
    down_grad = jnp.concatenate([low, high], axis=0)

    small = jnp.concatenate([head_local.T, gain_local[None, :]], axis=0)
    bit = 1
    while bit < count:
        small = small + flip(small, bit)
        bit *= 2
    small = small + other(small)
    head_grad = small[:-1].T
    gain_grad = small[-1]

    near, far, tied = lax.optimization_barrier((own_weight, far_weight, rounded))
    full_down = place_rows(near, far, order, half_rows)
    fresh_stream = fresh_residual.astype(f32) + jnp.dot(
        fresh_hidden, full_down, preferred_element_type=f32
    )
    fresh_policy = head_outputs(fresh_stream, head_matrix, gain_vector)
    hidden_sum = lax.dot_general(
        tied, full_down, (((1,), (1,)), ((), ())), preferred_element_type=f32
    )
    hidden_grad = hidden_sum.astype(bf16)
    return (fresh_policy, targets, hidden_grad, down_grad, head_grad, gain_grad)


def solution(mesh):
    placed = (
        P(("dp", "rep"), None),
        P(("dp", "rep"), None),
        P(("dp", "rep"), None),
        P(("dp", "rep"), None),
        P("dp", None),
        P(),
        P(),
        P(("dp", "rep"), None),
        P(("dp", "rep"), None),
        P(("dp", "rep"), None),
        P(("dp", "rep"), None),
        P(("dp", "rep")),
        P(("dp", "rep")),
    )
    count = mesh.shape["dp"]
    return jax.shard_map(
        functools.partial(local, count),
        mesh=mesh,
        in_specs=placed,
        out_specs=(
            P(("dp", "rep"), None),
            P(("dp", "rep"), None),
            P(("dp", "rep"), None),
            P("dp", None),
            P(),
            P(),
        ),
        check_vma=False,
    )
```

```python
import functools

import jax
import jax.numpy as jnp
from jax import lax
from jax.experimental import pallas as pl
from jax.experimental.pallas import tpu as pltpu
from jax.sharding import PartitionSpec as P

ACTIONS = 18
STEPS = 80
TRAJ_DEV = 8


DISCOUNT = 0.99
BASELINE_COST = 0.5
ENTROPY_COST = 0.05
EPSILON = 1e-05


def normalize(features, gain_vector):
    inverse_rms = lax.rsqrt(jnp.mean(features * features, axis=1, keepdims=True) + EPSILON)
    return features * inverse_rms * gain_vector[None, :]


def head_outputs(features, head_matrix, gain_vector):
    return jnp.dot(normalize(features, gain_vector), head_matrix, precision=lax.Precision.HIGHEST)


def log_policy(logits):
    return logits - jnp.log(jnp.sum(jnp.exp(logits), axis=-1, keepdims=True))


def compose_steps(earlier, later):
    return (earlier[0] * later[0], later[1] + later[0] * earlier[1])


def trace_returns(errors, traces):
    _, corrections = lax.associative_scan(compose_steps, (traces, errors), reverse=True, axis=1)
    return corrections


def learner_loss(
    features,
    head_matrix,
    gain_vector,
    actions,
    behaviour_logits,
    rewards,
    episode_done,
    lengths,
    bootstrap,
):
    trajectories = actions.shape[0]
    outputs = head_outputs(features, head_matrix, gain_vector)
    logprob = log_policy(outputs[:, :ACTIONS])
    values = outputs[:, ACTIONS].reshape(trajectories, STEPS)
    one_hot = (
        actions.reshape(-1)[:, None] == jnp.arange(ACTIONS, dtype=jnp.int32)[None, :]
    ).astype(jnp.float32)
    taken = jnp.sum(logprob * one_hot, axis=1).reshape(trajectories, STEPS)
    behaved = jnp.sum(log_policy(behaviour_logits) * one_hot, axis=1).reshape(trajectories, STEPS)
    entropy = -jnp.sum(jnp.exp(logprob) * logprob, axis=1).reshape(trajectories, STEPS)
    clipped_ratio = jnp.minimum(1.0, jnp.exp(lax.stop_gradient(taken) - behaved))
    positions = jnp.arange(STEPS, dtype=jnp.int32)[None, :]
    inside = positions < lengths[:, None]
    final_step = positions == lengths[:, None] - 1
    discounts = DISCOUNT * (1.0 - episode_done.astype(jnp.float32))
    baseline = lax.stop_gradient(values)
    empty_column = jnp.zeros((trajectories, 1), jnp.float32)
    next_value = jnp.concatenate([baseline[:, 1:], empty_column], axis=1)
    next_value = jnp.where(final_step, bootstrap[:, None], next_value)
    errors = jnp.where(inside, clipped_ratio * (rewards + discounts * next_value - baseline), 0.0)
    traces = jnp.where(inside, discounts * clipped_ratio, 0.0)
    targets = baseline + trace_returns(errors, traces)
    next_target = jnp.concatenate([targets[:, 1:], empty_column], axis=1)
    next_target = jnp.where(final_step, bootstrap[:, None], next_target)
    advantage = clipped_ratio * (rewards + discounts * next_target - baseline)
    per_step = (
        -advantage * taken + 0.5 * BASELINE_COST * (targets - values) ** 2 - ENTROPY_COST * entropy
    )
    total_loss = jnp.sum(jnp.where(inside, per_step, 0.0)) / (TRAJ_DEV * STEPS)
    return (total_loss, targets)


MESH = pl.DeviceIdType.MESH


def gather_kernel(count, mine, whole, send, recv, ring_send, ring_recv, local_sem):
    slow = count // 4
    rows = mine.shape[0]
    half, quarter = rows // 2, rows // 4
    me = lax.axis_index("dp")
    my_rep = lax.axis_index("rep")
    my_slow, my_mid, my_core = me // 4, (me // 2) % 2, me % 2

    def at(slow_at, mid_at, core_at):
        return slow_at * 4 + mid_at * 2 + core_at

    to_ring = {"dp": at((my_slow + slow - 1) % slow, my_mid, my_core)}
    from_ring = {"dp": at((my_slow + 1) % slow, my_mid, my_core)}
    to_mid = {"dp": at(my_slow, 1 - my_mid, my_core)}
    to_core = {"dp": at(my_slow, my_mid, 1 - my_core)}
    to_rep = {"rep": 1 - my_rep}

    barrier = pltpu.get_barrier_semaphore()
    for peer in (to_ring, from_ring, to_mid, to_core, to_rep):
        pl.semaphore_signal(barrier, inc=1, device_id=peer, device_id_type=MESH)
    pl.semaphore_wait(barrier, 5)

    def spot(start, size):
        return pl.ds(pl.multiple_of(start, quarter), size)

    def begin(source_own, start, size, send_sem, recv_sem, peer):
        inside = start - me * rows
        source = mine.at[spot(inside, size)] if source_own else whole.at[spot(start, size)]
        copy = pltpu.make_async_remote_copy(
            src_ref=source,
            dst_ref=whole.at[spot(start, size)],
            send_sem=send_sem,
            recv_sem=recv_sem,
            device_id=peer,
            device_id_type=MESH,
        )
        copy.start()
        return copy

    def block_start(s, mid_at):
        return at((my_slow + s) % slow, mid_at, my_core) * rows

    keep = pltpu.make_async_copy(mine, whole.at[spot(me * rows, rows)], local_sem)
    keep.start()
    copies = {}
    sent = []

    def go(kind, s, start, size, peer, own):
        copy = begin(own, start, size, send.at[s, kind], recv.at[s, kind], peer)
        copies[s, kind] = copy
        sent.append(copy)

    def ring(s):
        start = block_start(s, my_mid) + my_rep * half
        copy = begin(s == 0, start, half, ring_send.at[s], ring_recv.at[s], to_ring)
        copies[s, "ring"] = copy
        sent.append(copy)

    def first(s):
        base = block_start(s, my_mid)
        if s > 0:
            copies[s - 1, "ring"].wait_recv()
        if s < slow - 1:
            ring(s)
        go(3, s, base + my_rep * half + quarter, quarter, to_mid, s == 0)
        if s > 0:
            go(0, s, base + my_rep * half, quarter, to_rep, False)

    def second(s):
        base, beside = block_start(s, my_mid), block_start(s, 1 - my_mid)
        go(1, s, base + my_rep * half, quarter, to_mid, s == 0)
        if s > 0:
            go(4, s, base + my_rep * half + quarter, quarter, to_rep, False)
            copies[s, 0].wait_recv()
        go(2, s, base + (1 - my_rep) * half, quarter, to_mid, s == 0)
        copies[s, 3].wait_recv()
        go(5, s, beside + my_rep * half + quarter, quarter, to_rep, False)

    def third(s):
        if s > 0:
            copies[s, 4].wait_recv()
        go(6, s, block_start(s, my_mid), rows, to_core, s == 0)
        copies[s, 1].wait_recv()
        copies[s, 2].wait_recv()
        copies[s, 5].wait_recv()
        go(7, s, block_start(s, 1 - my_mid), rows, to_core, False)

    for s in range(slow + 2):
        if s < slow:
            first(s)
        if 0 <= s - 1 < slow:
            second(s - 1)
        if 0 <= s - 2 < slow:
            third(s - 2)
    keep.wait()
    for s in range(slow):
        copies[s, 6].wait_recv()
        copies[s, 7].wait_recv()
    for copy in sent:
        copy.wait_send()


def gather_rows(count, block):
    rows, width = block.shape
    slow = count // 4
    return pl.pallas_call(
        functools.partial(gather_kernel, count),
        out_shape=jax.ShapeDtypeStruct((count * rows, width), block.dtype),
        in_specs=[pl.BlockSpec(memory_space=pltpu.VMEM)],
        out_specs=pl.BlockSpec(memory_space=pl.ANY),
        scratch_shapes=[
            pltpu.SemaphoreType.DMA((slow, 8)),
            pltpu.SemaphoreType.DMA((slow, 8)),
            pltpu.SemaphoreType.DMA((slow,)),
            pltpu.SemaphoreType.DMA((slow,)),
            pltpu.SemaphoreType.DMA,
        ],
        compiler_params=pltpu.CompilerParams(collective_id=0, has_side_effects=True),
    )(block)


def grad_kernel(order_ref, h0, h1, h2, h3, grad_ref, first_ref, second_ref):
    width = h0.shape[1]
    cols = first_ref.shape[1]
    for k, hidden in enumerate((h0, h1, h2, h3)):
        product = lax.dot_general(
            hidden[...],
            grad_ref[...],
            (((0,), (0,)), ((), ())),
            preferred_element_type=jnp.float32,
        )
        rows = pl.ds(k * width, width)
        first_ref[rows, :] = product[:, :cols].astype(first_ref.dtype)
        second_ref[rows, :] = product[:, cols:].astype(second_ref.dtype)


def grad_blocks(hidden, grad, order, width, dtype):
    rows, total = hidden.shape
    many = order.shape[0]
    cols = grad.shape[1] // 2
    if width % 128 or many % 4:
        picked = jnp.take(hidden.reshape(rows, total // width, width), order, axis=1)
        product = lax.dot_general(
            picked.reshape(rows, many * width),
            grad,
            (((0,), (0,)), ((), ())),
            preferred_element_type=jnp.float32,
        ).astype(dtype)
        return product[:, :cols], product[:, cols:]
    out = jax.ShapeDtypeStruct((many * width, cols), dtype)
    spec = pl.BlockSpec((4 * width, cols), lambda j, index: (j, 0))
    return pl.pallas_call(
        grad_kernel,
        out_shape=(out, out),
        grid_spec=pltpu.PrefetchScalarGridSpec(
            num_scalar_prefetch=1,
            grid=(many // 4,),
            in_specs=[
                pl.BlockSpec((rows, width), lambda j, index: (0, index[4 * j])),
                pl.BlockSpec((rows, width), lambda j, index: (0, index[4 * j + 1])),
                pl.BlockSpec((rows, width), lambda j, index: (0, index[4 * j + 2])),
                pl.BlockSpec((rows, width), lambda j, index: (0, index[4 * j + 3])),
                pl.BlockSpec(grad.shape, lambda j, index: (0, 0)),
            ],
            out_specs=(spec, spec),
        ),
        cost_estimate=pl.CostEstimate(
            flops=4 * rows * many * width * cols,
            bytes_accessed=2 * rows * many * width + 4 * many * width * cols,
            transcendentals=0,
        ),
    )(order, hidden, hidden, hidden, hidden, grad)


def local(count, learn_residual,
    learn_hidden,
    fresh_residual,
    fresh_hidden,
    down_weight,
    head_weight,
    norm_gain,
    actions,
    behaviour_logits,
    rewards,
    episode_done,
    lengths,
    bootstrap):
    slow = count // 4
    half_rows = down_weight.shape[0] // 2
    width = down_weight.shape[1]
    cols = width // 2
    bf16, f32 = jnp.bfloat16, jnp.float32

    def flip(array, bit):
        return lax.ppermute(array, "dp", [(i, i ^ bit) for i in range(count)])

    def turn(array, steps):
        return lax.ppermute(array, "dp", [(i, (i + 4 * steps) % count) for i in range(count)])

    def other(array):
        return lax.ppermute(array, "rep", [(0, 1), (1, 0)])

    me = lax.axis_index("dp")
    my_rep = lax.axis_index("rep")
    my_slow, my_mid, my_core = me // 4, (me // 2) % 2, me % 2
    place = jnp.arange(count * 2, dtype=jnp.int32)
    s_slow = place % slow
    s_rep = (place // slow) % 2
    s_mid = (place // (slow * 2)) % 2
    s_core = place // (slow * 4)
    block = ((my_slow + s_slow) % slow) * 4 + ((my_mid + s_mid) % 2) * 2 + (my_core + s_core) % 2
    order = (block * 2 + (my_rep + s_rep) % 2).astype(jnp.int32)

    head_matrix = head_weight.astype(f32)
    gain_vector = norm_gain.astype(f32)
    full_down = gather_rows(count, down_weight)
    step = slow * half_rows
    depth = count * half_rows
    learn_stream = learn_residual.astype(f32) + jnp.dot(
        learn_hidden, full_down, preferred_element_type=f32
    )

    def loss_of(features, head_values, gain_values):
        return learner_loss(
            features,
            head_values,
            gain_values,
            actions,
            behaviour_logits,
            rewards,
            episode_done,
            lengths,
            bootstrap,
        )

    total_loss, pullback, targets = jax.vjp(
        loss_of, learn_stream, head_matrix, gain_vector, has_aux=True
    )
    stream_grad, head_local, gain_local = pullback(jnp.ones_like(total_loss))
    rounded = stream_grad.astype(bf16)

    far = grad_blocks(learn_hidden, rounded, order[count:], half_rows, bf16)
    sent = [flip(side, 1) for side in far]
    near = grad_blocks(learn_hidden, rounded, order[:count], half_rows, f32)
    a, b = (side + got.astype(f32) for side, got in zip(near, sent))
    a = a.reshape(2, 2, step, cols)
    b = b.reshape(2, 2, step, cols)
    a_got = flip(a[1].astype(bf16), 2)
    b_got = other(b[:, 1].astype(bf16))
    a = a[0] + a_got.astype(f32)
    b = b[:, 0] + b_got.astype(f32)
    a_got = other(a[1].astype(bf16))
    b_got = flip(b[1].astype(bf16), 2)
    a = a[0] + a_got.astype(f32)
    b = b[0] + b_got.astype(f32)
    done = []
    for whole in (a, b):
        whole = whole.reshape(slow, half_rows, cols)
        narrow = whole.astype(bf16)
        arrived = [turn(narrow[s], s) for s in range(1, slow)]
        total = whole[0]
        for got in arrived:
            total = total + got.astype(f32)
        done.append(lax.reduce_precision(total, 8, 7))
    mine = jnp.concatenate(done, axis=1)
    theirs = other(mine.astype(bf16)).astype(f32)
    low = jnp.where(my_rep == 0, mine, theirs)
    high = jnp.where(my_rep == 0, theirs, mine)
    down_grad = jnp.concatenate([low, high], axis=0)

    small = jnp.concatenate([head_local.T, gain_local[None, :]], axis=0)
    bit = 1
    while bit < count:
        small = small + flip(small, bit)
        bit *= 2
    small = small + other(small)
    head_grad = small[:-1].T
    gain_grad = small[-1]

    later_hidden, tied = lax.optimization_barrier((fresh_hidden, rounded))
    fresh_stream = fresh_residual.astype(f32) + jnp.dot(
        later_hidden, full_down, preferred_element_type=f32
    )
    fresh_policy = head_outputs(fresh_stream, head_matrix, gain_vector)
    hidden_sum = lax.dot_general(
        tied, full_down, (((1,), (1,)), ((), ())), preferred_element_type=f32
    )
    hidden_grad = hidden_sum.astype(bf16)
    return (fresh_policy, targets, hidden_grad, down_grad, head_grad, gain_grad)


def solution(mesh):
    placed = (
        P(("dp", "rep"), None),
        P(("dp", "rep"), None),
        P(("dp", "rep"), None),
        P(("dp", "rep"), None),
        P("dp", None),
        P(),
        P(),
        P(("dp", "rep"), None),
        P(("dp", "rep"), None),
        P(("dp", "rep"), None),
        P(("dp", "rep"), None),
        P(("dp", "rep")),
        P(("dp", "rep")),
    )
    count = mesh.shape["dp"]
    return jax.shard_map(
        functools.partial(local, count),
        mesh=mesh,
        in_specs=placed,
        out_specs=(
            P(("dp", "rep"), None),
            P(("dp", "rep"), None),
            P(("dp", "rep"), None),
            P("dp", None),
            P(),
            P(),
        ),
        check_vma=False,
    )
```

```python
import functools

import jax
import jax.numpy as jnp
from jax import lax
from jax.experimental import pallas as pl
from jax.experimental.pallas import tpu as pltpu
from jax.sharding import PartitionSpec as P

ACTIONS = 18
STEPS = 80
TRAJ_DEV = 8


DISCOUNT = 0.99
BASELINE_COST = 0.5
ENTROPY_COST = 0.05
EPSILON = 1e-05


def normalize(features, gain_vector):
    inverse_rms = lax.rsqrt(jnp.mean(features * features, axis=1, keepdims=True) + EPSILON)
    return features * inverse_rms * gain_vector[None, :]


def head_outputs(features, head_matrix, gain_vector):
    return jnp.dot(normalize(features, gain_vector), head_matrix, precision=lax.Precision.HIGHEST)


def log_policy(logits):
    return logits - jnp.log(jnp.sum(jnp.exp(logits), axis=-1, keepdims=True))


def compose_steps(earlier, later):
    return (earlier[0] * later[0], later[1] + later[0] * earlier[1])


def trace_returns(errors, traces):
    _, corrections = lax.associative_scan(compose_steps, (traces, errors), reverse=True, axis=1)
    return corrections


def learner_loss(
    features,
    head_matrix,
    gain_vector,
    actions,
    behaviour_logits,
    rewards,
    episode_done,
    lengths,
    bootstrap,
):
    trajectories = actions.shape[0]
    outputs = head_outputs(features, head_matrix, gain_vector)
    logprob = log_policy(outputs[:, :ACTIONS])
    values = outputs[:, ACTIONS].reshape(trajectories, STEPS)
    one_hot = (
        actions.reshape(-1)[:, None] == jnp.arange(ACTIONS, dtype=jnp.int32)[None, :]
    ).astype(jnp.float32)
    taken = jnp.sum(logprob * one_hot, axis=1).reshape(trajectories, STEPS)
    behaved = jnp.sum(log_policy(behaviour_logits) * one_hot, axis=1).reshape(trajectories, STEPS)
    entropy = -jnp.sum(jnp.exp(logprob) * logprob, axis=1).reshape(trajectories, STEPS)
    clipped_ratio = jnp.minimum(1.0, jnp.exp(lax.stop_gradient(taken) - behaved))
    positions = jnp.arange(STEPS, dtype=jnp.int32)[None, :]
    inside = positions < lengths[:, None]
    final_step = positions == lengths[:, None] - 1
    discounts = DISCOUNT * (1.0 - episode_done.astype(jnp.float32))
    baseline = lax.stop_gradient(values)
    empty_column = jnp.zeros((trajectories, 1), jnp.float32)
    next_value = jnp.concatenate([baseline[:, 1:], empty_column], axis=1)
    next_value = jnp.where(final_step, bootstrap[:, None], next_value)
    errors = jnp.where(inside, clipped_ratio * (rewards + discounts * next_value - baseline), 0.0)
    traces = jnp.where(inside, discounts * clipped_ratio, 0.0)
    targets = baseline + trace_returns(errors, traces)
    next_target = jnp.concatenate([targets[:, 1:], empty_column], axis=1)
    next_target = jnp.where(final_step, bootstrap[:, None], next_target)
    advantage = clipped_ratio * (rewards + discounts * next_target - baseline)
    per_step = (
        -advantage * taken + 0.5 * BASELINE_COST * (targets - values) ** 2 - ENTROPY_COST * entropy
    )
    total_loss = jnp.sum(jnp.where(inside, per_step, 0.0)) / (TRAJ_DEV * STEPS)
    return (total_loss, targets)


MESH = pl.DeviceIdType.MESH


def gather_kernel(count, mine, whole, send, recv, ring_send, ring_recv, local_sem):
    slow = count // 4
    rows = mine.shape[0]
    half, quarter = rows // 2, rows // 4
    me = lax.axis_index("dp")
    my_rep = lax.axis_index("rep")
    my_slow, my_mid, my_core = me // 4, (me // 2) % 2, me % 2

    def at(slow_at, mid_at, core_at):
        return slow_at * 4 + mid_at * 2 + core_at

    to_ring = {"dp": at((my_slow + slow - 1) % slow, my_mid, my_core)}
    from_ring = {"dp": at((my_slow + 1) % slow, my_mid, my_core)}
    to_mid = {"dp": at(my_slow, 1 - my_mid, my_core)}
    to_core = {"dp": at(my_slow, my_mid, 1 - my_core)}
    to_rep = {"rep": 1 - my_rep}

    barrier = pltpu.get_barrier_semaphore()
    for peer in (to_ring, from_ring, to_mid, to_core, to_rep):
        pl.semaphore_signal(barrier, inc=1, device_id=peer, device_id_type=MESH)
    pl.semaphore_wait(barrier, 5)

    def spot(start, size):
        return pl.ds(pl.multiple_of(start, quarter), size)

    def begin(source_own, start, size, send_sem, recv_sem, peer):
        inside = start - me * rows
        source = mine.at[spot(inside, size)] if source_own else whole.at[spot(start, size)]
        copy = pltpu.make_async_remote_copy(
            src_ref=source,
            dst_ref=whole.at[spot(start, size)],
            send_sem=send_sem,
            recv_sem=recv_sem,
            device_id=peer,
            device_id_type=MESH,
        )
        copy.start()
        return copy

    def block_start(s, mid_at):
        return at((my_slow + s) % slow, mid_at, my_core) * rows

    keep = pltpu.make_async_copy(mine, whole.at[spot(me * rows, rows)], local_sem)
    keep.start()
    copies = {}
    sent = []

    def go(kind, s, start, size, peer, own):
        copy = begin(own, start, size, send.at[s, kind], recv.at[s, kind], peer)
        copies[s, kind] = copy
        sent.append(copy)

    def ring(s):
        start = block_start(s, my_mid) + my_rep * half
        copy = begin(s == 0, start, half, ring_send.at[s], ring_recv.at[s], to_ring)
        copies[s, "ring"] = copy
        sent.append(copy)

    def first(s):
        base = block_start(s, my_mid)
        if s > 0:
            copies[s - 1, "ring"].wait_recv()
        if s < slow - 1:
            ring(s)
        go(3, s, base + my_rep * half + quarter, quarter, to_mid, s == 0)
        if s > 0:
            go(0, s, base + my_rep * half, quarter, to_rep, False)

    def second(s):
        base, beside = block_start(s, my_mid), block_start(s, 1 - my_mid)
        go(1, s, base + my_rep * half, quarter, to_mid, s == 0)
        if s > 0:
            go(4, s, base + my_rep * half + quarter, quarter, to_rep, False)
            copies[s, 0].wait_recv()
        go(2, s, base + (1 - my_rep) * half, quarter, to_mid, s == 0)
        copies[s, 3].wait_recv()
        go(5, s, beside + my_rep * half + quarter, quarter, to_rep, False)

    def third(s):
        if s > 0:
            copies[s, 4].wait_recv()
        go(6, s, block_start(s, my_mid), rows, to_core, s == 0)
        copies[s, 1].wait_recv()
        copies[s, 2].wait_recv()
        copies[s, 5].wait_recv()
        go(7, s, block_start(s, 1 - my_mid), rows, to_core, False)

    for s in range(slow + 2):
        if s < slow:
            first(s)
        if 0 <= s - 1 < slow:
            second(s - 1)
        if 0 <= s - 2 < slow:
            third(s - 2)
    keep.wait()
    for s in range(slow):
        copies[s, 6].wait_recv()
        copies[s, 7].wait_recv()
    for copy in sent:
        copy.wait_send()


def gather_rows(count, block):
    rows, width = block.shape
    slow = count // 4
    return pl.pallas_call(
        functools.partial(gather_kernel, count),
        out_shape=jax.ShapeDtypeStruct((count * rows, width), block.dtype),
        in_specs=[pl.BlockSpec(memory_space=pltpu.VMEM)],
        out_specs=pl.BlockSpec(memory_space=pl.ANY),
        scratch_shapes=[
            pltpu.SemaphoreType.DMA((slow, 8)),
            pltpu.SemaphoreType.DMA((slow, 8)),
            pltpu.SemaphoreType.DMA((slow,)),
            pltpu.SemaphoreType.DMA((slow,)),
            pltpu.SemaphoreType.DMA,
        ],
        compiler_params=pltpu.CompilerParams(collective_id=0, has_side_effects=True),
    )(block)


def grad_kernel(order_ref, h0, h1, h2, h3, grad_ref, first_ref, second_ref):
    width = h0.shape[1]
    cols = first_ref.shape[1]
    for k, hidden in enumerate((h0, h1, h2, h3)):
        product = lax.dot_general(
            hidden[...],
            grad_ref[...],
            (((0,), (0,)), ((), ())),
            preferred_element_type=jnp.float32,
        )
        rows = pl.ds(k * width, width)
        first_ref[rows, :] = product[:, :cols].astype(first_ref.dtype)
        second_ref[rows, :] = product[:, cols:].astype(second_ref.dtype)


def grad_blocks(hidden, grad, order, width, dtype):
    rows, total = hidden.shape
    many = order.shape[0]
    cols = grad.shape[1] // 2
    if width % 128 or many % 4:
        picked = jnp.take(hidden.reshape(rows, total // width, width), order, axis=1)
        product = lax.dot_general(
            picked.reshape(rows, many * width),
            grad,
            (((0,), (0,)), ((), ())),
            preferred_element_type=jnp.float32,
        ).astype(dtype)
        return product[:, :cols], product[:, cols:]
    out = jax.ShapeDtypeStruct((many * width, cols), dtype)
    spec = pl.BlockSpec((4 * width, cols), lambda j, index: (j, 0))
    return pl.pallas_call(
        grad_kernel,
        out_shape=(out, out),
        grid_spec=pltpu.PrefetchScalarGridSpec(
            num_scalar_prefetch=1,
            grid=(many // 4,),
            in_specs=[
                pl.BlockSpec((rows, width), lambda j, index: (0, index[4 * j])),
                pl.BlockSpec((rows, width), lambda j, index: (0, index[4 * j + 1])),
                pl.BlockSpec((rows, width), lambda j, index: (0, index[4 * j + 2])),
                pl.BlockSpec((rows, width), lambda j, index: (0, index[4 * j + 3])),
                pl.BlockSpec(grad.shape, lambda j, index: (0, 0)),
            ],
            out_specs=(spec, spec),
        ),
        cost_estimate=pl.CostEstimate(
            flops=4 * rows * many * width * cols,
            bytes_accessed=2 * rows * many * width + 4 * many * width * cols,
            transcendentals=0,
        ),
    )(order, hidden, hidden, hidden, hidden, grad)


def reduce_kernel(
    count, half_rows, near_a, near_b, got_a, got_b, out,
    send1, recv1, send2, recv2, send3, recv3, keep, last_send, last_recv,
    s1_send, s1_recv, s2_send, s2_recv, s3_send, s3_recv, s4_send, s4_recv,
):
    slow = count // 4
    me = lax.axis_index("dp")
    my_rep = lax.axis_index("rep")
    my_slow, my_mid, my_core = me // 4, (me // 2) % 2, me % 2
    cols = near_a.shape[1]
    to_mid = {"dp": my_slow * 4 + (1 - my_mid) * 2 + my_core}
    to_rep = {"rep": 1 - my_rep}

    def to_slow(s):
        return {"dp": ((my_slow + s) % slow) * 4 + my_mid * 2 + my_core}

    barrier = pltpu.get_barrier_semaphore()
    for peer in [to_mid, to_rep] + [to_slow(s) for s in range(1, slow)]:
        pl.semaphore_signal(barrier, inc=1, device_id=peer, device_id_type=MESH)
    pl.semaphore_wait(barrier, slow + 1)

    near, got = (near_a, near_b), (got_a, got_b)
    copies = {}

    def load(side, mid, rep, s):
        rows = pl.ds(((mid * 2 + rep) * slow + s) * half_rows, half_rows)
        return near[side][rows, :] + got[side][rows, :].astype(jnp.float32)

    def go(key, source, target, send_sem, recv_sem, peer):
        copy = pltpu.make_async_remote_copy(
            src_ref=source,
            dst_ref=target,
            send_sem=send_sem,
            recv_sem=recv_sem,
            device_id=peer,
            device_id_type=MESH,
        )
        copy.start()
        copies[key] = copy

    def stage1(s):
        for late in (1, 0):
            for side, peer in ((0, to_mid), (1, to_rep)):
                mid, rep = (1, late) if side == 0 else (late, 1)
                slot = side * 2 + late
                send1[s, slot] = load(side, mid, rep, s).astype(jnp.bfloat16)
                go(
                    (1, s, slot), send1.at[s, slot], recv1.at[s, slot],
                    s1_send.at[s, slot], s1_recv.at[s, slot], peer,
                )

    def stage2(s):
        for side, peer in ((0, to_rep), (1, to_mid)):
            mid, rep = (0, 1) if side == 0 else (1, 0)
            slot = side * 2 + 1
            copies[1, s, slot].wait_recv()
            total = load(side, mid, rep, s) + recv1[s, slot].astype(jnp.float32)
            send2[s, side] = total.astype(jnp.bfloat16)
            go(
                (2, s, side), send2.at[s, side], recv2.at[s, side],
                s2_send.at[s, side], s2_recv.at[s, side], peer,
            )

    def stage3(s):
        for side in (0, 1):
            copies[1, s, side * 2].wait_recv()
            copies[2, s, side].wait_recv()
            total = (
                load(side, 0, 0, s)
                + recv1[s, side * 2].astype(jnp.float32)
                + recv2[s, side].astype(jnp.float32)
            )
            if s == 0:
                keep[side] = total
                continue
            send3[s, side] = total.astype(jnp.bfloat16)
            go(
                (3, s, side), send3.at[s, side], recv3.at[s, side],
                s3_send.at[s, side], s3_recv.at[s, side], to_slow(s),
            )

    turns = list(range(1, slow)) + [0]
    for step in range(slow + 2):
        if step < slow:
            stage1(turns[step])
        if 0 <= step - 1 < slow:
            stage2(turns[step - 1])
        if 0 <= step - 2 < slow:
            stage3(turns[step - 2])
    for side in (0, 1):
        total = keep[side]
        for s in range(1, slow):
            copies[3, s, side].wait_recv()
            total = total + recv3[s, side].astype(jnp.float32)
        last_send[side] = total.astype(jnp.bfloat16)
        go(
            (4, side), last_send.at[side], last_recv.at[side],
            s4_send.at[side], s4_recv.at[side], to_rep,
        )
    mine = pl.ds(pl.multiple_of(my_rep * half_rows, half_rows), half_rows)
    theirs = pl.ds(pl.multiple_of((1 - my_rep) * half_rows, half_rows), half_rows)
    for side in (0, 1):
        out[mine, pl.ds(side * cols, cols)] = last_send[side].astype(jnp.float32)
    for side in (0, 1):
        copies[4, side].wait_recv()
        out[theirs, pl.ds(side * cols, cols)] = last_recv[side].astype(jnp.float32)
    for copy in copies.values():
        copy.wait_send()


def reduce_rows(count, half_rows, near, got):
    slow = count // 4
    cols = near[0].shape[1]
    bf16 = jnp.bfloat16
    dma = pltpu.SemaphoreType.DMA

    def buffer(*lead):
        return pltpu.VMEM((*lead, half_rows, cols), bf16)

    return pl.pallas_call(
        functools.partial(reduce_kernel, count, half_rows),
        out_shape=jax.ShapeDtypeStruct((2 * half_rows, 2 * cols), jnp.float32),
        in_specs=[pl.BlockSpec(memory_space=pltpu.VMEM)] * 4,
        out_specs=pl.BlockSpec(memory_space=pltpu.VMEM),
        scratch_shapes=[
            buffer(slow, 4), buffer(slow, 4),
            buffer(slow, 2), buffer(slow, 2),
            buffer(slow, 2), buffer(slow, 2),
            pltpu.VMEM((2, half_rows, cols), jnp.float32),
            buffer(2), buffer(2),
            dma((slow, 4)), dma((slow, 4)),
            dma((slow, 2)), dma((slow, 2)),
            dma((slow, 2)), dma((slow, 2)),
            dma((2,)), dma((2,)),
        ],
        compiler_params=pltpu.CompilerParams(collective_id=1, has_side_effects=True),
    )(*near, *got)


def local(count, learn_residual,
    learn_hidden,
    fresh_residual,
    fresh_hidden,
    down_weight,
    head_weight,
    norm_gain,
    actions,
    behaviour_logits,
    rewards,
    episode_done,
    lengths,
    bootstrap):
    slow = count // 4
    half_rows = down_weight.shape[0] // 2
    width = down_weight.shape[1]
    cols = width // 2
    bf16, f32 = jnp.bfloat16, jnp.float32

    def flip(array, bit):
        return lax.ppermute(array, "dp", [(i, i ^ bit) for i in range(count)])

    def other(array):
        return lax.ppermute(array, "rep", [(0, 1), (1, 0)])

    me = lax.axis_index("dp")
    my_rep = lax.axis_index("rep")
    my_slow, my_mid, my_core = me // 4, (me // 2) % 2, me % 2
    place = jnp.arange(count * 2, dtype=jnp.int32)
    s_slow = place % slow
    s_rep = (place // slow) % 2
    s_mid = (place // (slow * 2)) % 2
    s_core = place // (slow * 4)
    block = ((my_slow + s_slow) % slow) * 4 + ((my_mid + s_mid) % 2) * 2 + (my_core + s_core) % 2
    order = (block * 2 + (my_rep + s_rep) % 2).astype(jnp.int32)

    head_matrix = head_weight.astype(f32)
    gain_vector = norm_gain.astype(f32)
    full_down = gather_rows(count, down_weight)
    step = slow * half_rows
    depth = count * half_rows
    learn_stream = learn_residual.astype(f32) + jnp.dot(
        learn_hidden, full_down, preferred_element_type=f32
    )

    def loss_of(features, head_values, gain_values):
        return learner_loss(
            features,
            head_values,
            gain_values,
            actions,
            behaviour_logits,
            rewards,
            episode_done,
            lengths,
            bootstrap,
        )

    total_loss, pullback, targets = jax.vjp(
        loss_of, learn_stream, head_matrix, gain_vector, has_aux=True
    )
    stream_grad, head_local, gain_local = pullback(jnp.ones_like(total_loss))
    rounded = stream_grad.astype(bf16)

    far = grad_blocks(learn_hidden, rounded, order[count:], half_rows, bf16)
    sent = [flip(side, 1) for side in far]
    near = grad_blocks(learn_hidden, rounded, order[:count], half_rows, f32)
    down_grad = reduce_rows(count, half_rows, near, sent)

    small = jnp.concatenate([head_local.T, gain_local[None, :]], axis=0)
    bit = 1
    while bit < count:
        small = small + flip(small, bit)
        bit *= 2
    small = small + other(small)
    head_grad = small[:-1].T
    gain_grad = small[-1]

    later_hidden, tied = lax.optimization_barrier((fresh_hidden, rounded))
    fresh_stream = fresh_residual.astype(f32) + jnp.dot(
        later_hidden, full_down, preferred_element_type=f32
    )
    fresh_policy = head_outputs(fresh_stream, head_matrix, gain_vector)
    hidden_sum = lax.dot_general(
        tied, full_down, (((1,), (1,)), ((), ())), preferred_element_type=f32
    )
    hidden_grad = hidden_sum.astype(bf16)
    return (fresh_policy, targets, hidden_grad, down_grad, head_grad, gain_grad)


def solution(mesh):
    placed = (
        P(("dp", "rep"), None),
        P(("dp", "rep"), None),
        P(("dp", "rep"), None),
        P(("dp", "rep"), None),
        P("dp", None),
        P(),
        P(),
        P(("dp", "rep"), None),
        P(("dp", "rep"), None),
        P(("dp", "rep"), None),
        P(("dp", "rep"), None),
        P(("dp", "rep")),
        P(("dp", "rep")),
    )
    count = mesh.shape["dp"]
    return jax.shard_map(
        functools.partial(local, count),
        mesh=mesh,
        in_specs=placed,
        out_specs=(
            P(("dp", "rep"), None),
            P(("dp", "rep"), None),
            P(("dp", "rep"), None),
            P("dp", None),
            P(),
            P(),
        ),
        check_vma=False,
    )
```
